32 devices in a mesh: row: 16 (over z, x, core), col: 2 (over y).
Axes of the slice: x: 2, y: 2, z: 4, core: 2. Of those that a mesh axis runs over, the one named last changes fastest.
Arguments:
- qkv: bfloat16 [256, 16, 3, 3072], P('row', 'col'), may hold values from -6 to 6
- cotangent: bfloat16 [256, 16, 3072], P('row', 'col'), may hold values from -6 to 6
- norm_gains: float32 [2, 128], replicated, may hold values from 0.1 to 1.9
- rel_table: float32 [24, 15, 15], replicated, may hold values from -6 to 250
- shifts: int32 [2], replicated, may hold values from 1 to 7
- mask_ids: int32 [256, 16], replicated, may hold values from 0 to 2
Outputs:
- attention: bfloat16 [256, 16, 3072], P('row', 'col')
- d_qkv: bfloat16 [256, 16, 3, 3072], P('row', 'col')
- d_gains: float32 [2, 128], replicated
- d_table: float32 [24, 15, 15], replicated
The draws below stay inside these ranges and needn't reach their ends.
All inputs are finite; a program needn't handle non-finite values.
Results may differ from the reference program's by a relative error of at most 0.0073.
Values may be sent and summed in bfloat16 or wider, within the bound.
A program may use at most 192 MiB of HBM per device.

```python
import math
import jax
import jax.numpy as jnp
from jax import lax

WIN = 8
NH = 24
HD = 128
FEATURES = 3072
SPAN = 15
ROWS = 256
COLS = 16


def draw_rel_table(key, part):
    base = jnp.clip(jax.random.normal(jax.random.fold_in(key, 11), (NH, SPAN, SPAN), jnp.float32), -6.0, 6.0)
    return base


def with_ends(array, own_key, low, top_value):
    spot = [jax.random.randint(jax.random.fold_in(own_key, axis), (), 0, length) for axis, length in enumerate(array.shape)]
    main_axis = array.shape.index(max(array.shape))
    next_to = spot[:main_axis] + [(spot[main_axis] + 1) % array.shape[main_axis]] + spot[main_axis + 1:]
    return array.at[tuple(spot)].set(low).at[tuple(next_to)].set(top_value)


def shard_levels(own_key, extent, shards, least, largest):
    def one(position, shards_of):
        steps = jax.random.uniform(jax.random.fold_in(jax.random.fold_in(own_key, 6), position), (shards_of,), jnp.float32, least / len(shards), largest / len(shards))
        return jnp.repeat(jnp.exp(steps), extent[position] // shards_of).reshape((-1,) + (1,) * (len(extent) - position - 1))

    gain = one(*shards[0])
    for cut in shards[1:]:
        gain = gain * one(*cut)
    return gain


def bell_draw(own_key, dims, scale, most, split=(), kind=jnp.bfloat16):
    array = scale * jax.random.normal(own_key, dims, jnp.float32)
    if split:
        array = array * shard_levels(own_key, dims, split, -0.22, 0.18)
    return jnp.clip(array, -most, most).astype(kind)


def setup_inputs(seed: int = 0) -> dict:
    seeds = jax.random.split(jax.random.key(seed), 7)
    qkv = bell_draw(seeds[0], (ROWS, COLS, 3, FEATURES), 1.0, 6.0, ((0, 16), (1, 2)))
    cotangent = bell_draw(seeds[1], (ROWS, COLS, FEATURES), 1.0, 6.0, ((0, 16), (1, 2)))
    norm_gains = jnp.clip(1.0 + 0.18 * jax.random.normal(seeds[2], (2, HD), jnp.float32), 0.1, 1.9)
    rel_table = draw_rel_table(jax.random.fold_in(seeds[6], 71), 0)
    shifts = jax.random.randint(seeds[4], (2,), 1, WIN).astype(jnp.int32)
    mask_ids = with_ends(jax.random.randint(seeds[5], (ROWS, COLS), 0, 3), jax.random.fold_in(seeds[5], 1), 0, 2).astype(jnp.int32)
    return {"qkv": qkv, "cotangent": cotangent, "norm_gains": norm_gains, "rel_table": rel_table, "shifts": shifts, "mask_ids": mask_ids}


EPSILON = 1e-06
NEG_FILL = -1e+30

def head_norm(inputs, gain_vec):
    values = inputs.astype(jnp.float32)
    average = lax.optimization_barrier(jnp.mean(values, axis=-1, keepdims=True))
    centred = values - average
    variance = lax.optimization_barrier(jnp.mean(centred * centred, axis=-1, keepdims=True))
    inv_sigma = lax.rsqrt(variance + EPSILON)
    x_hat = centred * inv_sigma
    return (x_hat, inv_sigma, (x_hat * gain_vec).astype(jnp.bfloat16))

def norm_back(x_hat, inv_sigma, d_normed, gain_vec):
    d_hat = d_normed * gain_vec
    first_mean = lax.optimization_barrier(jnp.mean(d_hat, axis=-1, keepdims=True))
    second_mean = lax.optimization_barrier(jnp.mean(d_hat * x_hat, axis=-1, keepdims=True))
    d_input = inv_sigma * (d_hat - first_mean - x_hat * second_mean)
    d_gain = lax.optimization_barrier(jnp.sum(d_normed * x_hat, axis=tuple(range(d_normed.ndim - 1))))
    return (d_input, d_gain)

def offset_table(window_size):
    span_count = 2 * window_size - 1
    places = jnp.arange(window_size * window_size, dtype=jnp.int32)
    row_pos = places // window_size
    col_pos = places % window_size
    code_grid = (row_pos[:, None] - row_pos[None, :] + window_size - 1) * span_count + (col_pos[:, None] - col_pos[None, :] + window_size - 1)
    codes = jnp.arange(span_count * span_count, dtype=jnp.int32)
    return (code_grid[:, :, None] == codes[None, None, :]).astype(jnp.float32)

def to_windows(field, window_size):
    row_count, col_count = (field.shape[0], field.shape[1])
    trailing = field.shape[2:]
    blocks = field.reshape((row_count // window_size, window_size, col_count // window_size, window_size) + trailing)
    blocks = jnp.moveaxis(blocks, 2, 1)
    return blocks.reshape((row_count // window_size * (col_count // window_size), window_size * window_size) + trailing)

def from_windows(blocks, window_size, row_count, col_count):
    trailing = blocks.shape[2:]
    field = blocks.reshape((row_count // window_size, col_count // window_size, window_size, window_size) + trailing)
    field = jnp.moveaxis(field, 1, 2)
    return field.reshape((row_count, col_count) + trailing)

def product(form, left, right):
    return jnp.einsum(form, left.astype(jnp.float32), right.astype(jnp.float32))

def window_core(q_norm, k_norm, values, grads, pos_bias, allowed, score_scale):
    scores = product('wqhd,wkhd->whqk', q_norm, k_norm) * score_scale + pos_bias[None]
    scores = jnp.where(allowed[:, None], scores, NEG_FILL)
    row_max = lax.optimization_barrier(jnp.max(scores, axis=-1, keepdims=True))
    weights = jnp.exp(scores - row_max)
    probs = weights / lax.optimization_barrier(jnp.sum(weights, axis=-1, keepdims=True))
    probs_b = probs.astype(jnp.bfloat16)
    output = product('whqk,wkhd->wqhd', probs_b, values)
    d_probs = product('wqhd,wkhd->whqk', grads, values)
    row_dot = lax.optimization_barrier(jnp.sum(probs * d_probs, axis=-1, keepdims=True))
    d_scores = probs * (d_probs - row_dot)
    d_scores_b = d_scores.astype(jnp.bfloat16)
    d_qnorm = product('whqk,wkhd->wqhd', d_scores_b, k_norm) * score_scale
    d_knorm = product('whqk,wqhd->wkhd', d_scores_b, q_norm) * score_scale
    d_value = product('whqk,wqhd->wkhd', probs_b, grads)
    return (output, d_qnorm, d_knorm, d_value, lax.optimization_barrier(jnp.sum(d_scores, axis=0)))

def reference(qkv, cotangent, norm_gains, rel_table, shifts, mask_ids):
    shift_row = shifts[0]
    shift_col = shifts[1]
    score_scale = 1.0 / math.sqrt(HD)
    one_hot = offset_table(WIN)
    pos_bias = jnp.einsum('hc,qkc->hqk', rel_table.reshape(NH, SPAN * SPAN), one_hot, precision=lax.Precision.HIGHEST)
    labels = jnp.roll(mask_ids, (-shift_row, -shift_col), (0, 1))

    def one_band(band_index):
        row_index = ((band_index * WIN + shift_row + jnp.arange(WIN, dtype=jnp.int32)) % ROWS).astype(jnp.int32)
        band_qkv = jnp.roll(jnp.take(qkv, row_index, axis=0), -shift_col, axis=1)
        band_grad = jnp.roll(jnp.take(cotangent, row_index, axis=0), -shift_col, axis=1)
        band_labels = lax.dynamic_slice_in_dim(labels, (band_index * WIN).astype(jnp.int32), WIN, 0)
        fields = band_qkv.reshape(WIN, COLS, 3, NH, HD)
        q_hat, q_inv, q_norm = head_norm(fields[:, :, 0], norm_gains[0])
        k_hat, k_inv, k_norm = head_norm(fields[:, :, 1], norm_gains[1])
        label_win = to_windows(band_labels, WIN)
        allowed = label_win[:, :, None] == label_win[:, None, :]
        output, d_qnorm, d_knorm, d_value, d_bias = window_core(to_windows(q_norm, WIN), to_windows(k_norm, WIN), to_windows(fields[:, :, 2], WIN), to_windows(band_grad.reshape(WIN, COLS, NH, HD), WIN), pos_bias, allowed, score_scale)
        output = from_windows(output, WIN, WIN, COLS)
        d_qnorm = from_windows(d_qnorm, WIN, WIN, COLS)
        d_knorm = from_windows(d_knorm, WIN, WIN, COLS)
        d_value = from_windows(d_value, WIN, WIN, COLS)
        d_query, dgain_q = norm_back(q_hat, q_inv, d_qnorm, norm_gains[0])
        d_key, dgain_k = norm_back(k_hat, k_inv, d_knorm, norm_gains[1])
        packed = jnp.stack([output, d_query, d_key, d_value], axis=2).reshape(WIN, COLS, 4, NH * HD).astype(jnp.bfloat16)
        return (packed, d_bias, jnp.stack([dgain_q, dgain_k]))
    packed, d_bias, d_gain = lax.map(one_band, jnp.arange(ROWS // WIN, dtype=jnp.int32))
    packed = jnp.roll(packed.reshape(ROWS, COLS, 4, NH * HD), (shift_row, shift_col), (0, 1))
    d_table = jnp.einsum('hqk,qkc->hc', lax.optimization_barrier(jnp.sum(d_bias, axis=0)), one_hot, precision=lax.Precision.HIGHEST)
    return (packed[:, :, 0], packed[:, :, 1:], lax.optimization_barrier(jnp.sum(d_gain, axis=0)), d_table.reshape(NH, SPAN, SPAN))
```

```python
import functools
import math

import jax
import jax.numpy as jnp
from jax import lax
from jax.experimental import pallas as pl
from jax.experimental.pallas import tpu as pltpu
from jax.sharding import PartitionSpec as P

EPSILON = 1e-06
NEG_FILL = -1e30
AXES = ("row", "col")


def offset_table(window_size):
    span_count = 2 * window_size - 1
    places = jnp.arange(window_size * window_size, dtype=jnp.int32)
    row_pos = places % window_size
    col_pos = places // window_size
    code_grid = (row_pos[:, None] - row_pos[None, :] + window_size - 1) * span_count + (
        col_pos[:, None] - col_pos[None, :] + window_size - 1
    )
    codes = jnp.arange(span_count * span_count, dtype=jnp.int32)
    return (code_grid[:, :, None] == codes[None, None, :]).astype(jnp.float32)


def strip_exchange(field, half, row_dir, col_dir, width, reverse):
    rows = lax.axis_size("row")
    cols = lax.axis_size("col")
    row_step = -row_dir if not reverse else row_dir
    col_step = -col_dir if not reverse else col_dir
    tile_cols, tile_rows = field.shape[1], field.shape[2]
    row_part = slice(0, half) if row_dir > 0 else slice(tile_rows - half, tile_rows)
    col_part = slice(0, width) if col_dir > 0 else slice(tile_cols - width, tile_cols)
    row_strip = field[:, :, row_part]
    col_strip = field[:, col_part]
    corner = field[:, col_part, row_part]
    row_pairs = [(a, (a + row_step) % rows) for a in range(rows)]
    col_pairs = [(a, (a + col_step) % cols) for a in range(cols)]
    both_pairs = [
        (a * cols + b, ((a + row_step) % rows) * cols + (b + col_step) % cols)
        for a in range(rows)
        for b in range(cols)
    ]
    col_strip = lax.ppermute(col_strip, "col", col_pairs)
    corner = lax.ppermute(corner, AXES, both_pairs)
    row_strip = lax.ppermute(row_strip, "row", row_pairs)
    room = half - width
    pads = ((0, 0), (0, room) if col_dir > 0 else (room, 0), (0, 0), (0, 0))
    return (row_strip, jnp.pad(col_strip, pads), jnp.pad(corner, pads))


def exchange(field, half, step_row, step_col, reverse):
    branches = []
    for row_dir in (1, -1):
        for col_dir in (1, -1):
            for width in range(1, half + 1):
                branches.append(
                    functools.partial(
                        strip_exchange,
                        half=half,
                        row_dir=row_dir,
                        col_dir=col_dir,
                        width=width,
                        reverse=reverse,
                    )
                )
    index = (
        jnp.where(step_row > 0, 0, 2 * half)
        + jnp.where(step_col > 0, 0, half)
        + jnp.maximum(jnp.abs(step_col), 1)
        - 1
    )
    return lax.switch(index, branches, field)


def foreign(position, step, extent):
    return (position < step) | (position >= extent + step)


def merged_column(own, row_halo, col_halo, corner, f, q, lanes, step_row, step_col, half):
    tile_cols, tile_rows = own.shape[1], own.shape[2]
    outside = foreign(q, step_col, tile_cols)
    slot = lax.rem(q, half)
    main = jnp.where(outside, col_halo[f, slot, :, lanes], own[f, q, :, lanes])
    main = main.astype(jnp.float32)
    side = jnp.where(outside, corner[f, slot, :, lanes], row_halo[f, q, :, lanes])
    side = side.astype(jnp.float32)
    side = jnp.concatenate([side] * (tile_rows // half), axis=0)
    row = lax.broadcasted_iota(jnp.int32, main.shape, 0)
    return jnp.where(foreign(row, step_row, tile_rows), side, main)


def attend_kernel(
    steps, own, row_halo, col_halo, corner, gains, bias, neg, out, dgain, dbias, *, heads, dim, half
):
    step_row, step_col = steps[0], steps[1]
    tile_cols, tile_rows = own.shape[1], own.shape[2]
    win = 2 * half
    scale = 1.0 / math.sqrt(dim)

    @pl.when(pl.program_id(0) == 0)
    def _():
        dgain[...] = jnp.zeros_like(dgain)

    where_from = [lax.rem(j + step_col + tile_cols, tile_cols) for j in range(tile_cols)]
    up = lax.rem(tile_rows - step_row, tile_rows)
    down = lax.rem(tile_rows + step_row, tile_rows)
    bands = tile_rows // win
    tokens = tile_rows * tile_cols
    dot = functools.partial(lax.dot_general, preferred_element_type=jnp.float32)
    gain_q, gain_k = gains[0:1, :], gains[1:2, :]

    for h in range(heads):
        lanes = pl.ds(h * dim, dim)
        fields = []
        for f in range(4):
            columns = [
                pltpu.roll(
                    merged_column(
                        own, row_halo, col_halo, corner, f, q, lanes, step_row, step_col, half
                    ),
                    up,
                    0,
                )
                for q in where_from
            ]
            fields.append(
                jnp.concatenate(
                    [c[b * win : (b + 1) * win] for b in range(bands) for c in columns], axis=0
                )
            )

        def normed(x, gain):
            centred = x - jnp.mean(x, axis=-1, keepdims=True)
            variance = jnp.mean(centred * centred, axis=-1, keepdims=True)
            inv = lax.rsqrt(variance + EPSILON)
            hat = centred * inv
            return hat, inv, (hat * gain).astype(jnp.bfloat16)

        q_hat, q_inv, qn = normed(fields[0], gain_q)
        k_hat, k_inv, kn = normed(fields[1], gain_k)
        v = fields[2].astype(jnp.bfloat16)
        cot = fields[3].astype(jnp.bfloat16)
        b = jnp.concatenate([bias[h]] * bands, axis=0)
        s = dot(qn, kn, (((1,), (1,)), ((), ()))) * scale + b + neg[...]
        e = jnp.exp(s - jnp.max(s, axis=-1, keepdims=True))
        p = e / jnp.sum(e, axis=-1, keepdims=True)
        pb = p.astype(jnp.bfloat16)
        att = dot(pb, v, (((1,), (0,)), ((), ())))
        dp = dot(cot, v, (((1,), (1,)), ((), ())))
        ds = p * (dp - jnp.sum(p * dp, axis=-1, keepdims=True))
        dsb = ds.astype(jnp.bfloat16)
        dqn = dot(dsb, kn, (((1,), (0,)), ((), ()))) * scale
        dkn = dot(dsb, qn, (((0,), (0,)), ((), ()))) * scale
        dv = dot(pb, cot, (((0,), (0,)), ((), ())))
        folded = ds[0 : tokens // bands]
        for band in range(1, bands):
            folded = folded + ds[band * (tokens // bands) : (band + 1) * (tokens // bands)]
        dbias[h] = folded

        def norm_back(hat, inv, dn, gain):
            g = dn * gain
            first = jnp.mean(g, axis=-1, keepdims=True)
            second = jnp.mean(g * hat, axis=-1, keepdims=True)
            return inv * (g - first - hat * second), jnp.sum(dn * hat, axis=0, keepdims=True)

        dq, gq = norm_back(q_hat, q_inv, dqn, gain_q)
        dk, gk = norm_back(k_hat, k_inv, dkn, gain_k)
        dgain[...] += jnp.concatenate([gq, gk], axis=0)
        for f, result in enumerate((att, dq, dk, dv)):
            for j, q in enumerate(where_from):
                parts = [
                    result[(bd * tile_cols + j) * win : (bd * tile_cols + j + 1) * win]
                    for bd in range(bands)
                ]
                column = pltpu.roll(jnp.concatenate(parts, axis=0), down, 0)
                out[f, q, :, lanes] = column.astype(jnp.bfloat16)


def merge_kernel(steps, own, row_halo, col_halo, corner, out, *, half):
    lanes = pl.ds(0, own.shape[3])
    for f in range(own.shape[0]):
        for q in range(own.shape[1]):
            out[f, q] = merged_column(
                own, row_halo, col_halo, corner, f, q, lanes, steps[0], steps[1], half
            ).astype(jnp.bfloat16)


def field_specs(tile_cols, tile_rows, half, width):
    shapes = (
        (4, tile_cols, tile_rows, width),
        (4, tile_cols, half, width),
        (4, half, tile_rows, width),
        (4, half, half, width),
    )
    return [pl.BlockSpec(shape, lambda i: (0, 0, 0, i)) for shape in shapes]


def local(qkv, cotangent, norm_gains, rel_table, shifts, mask_ids):
    tile_rows, tile_cols = qkv.shape[0], qkv.shape[1]
    feature_width = qkv.shape[3]
    head_count = rel_table.shape[0]
    dim = feature_width // head_count
    span_count = rel_table.shape[1]
    win = (span_count + 1) // 2
    half = win // 2
    bands = tile_rows // win
    step = jnp.where(shifts <= half, shifts, shifts - win).astype(jnp.int32)

    field = jnp.concatenate([qkv, cotangent[:, :, None]], axis=2).transpose(2, 1, 0, 3)
    halos = exchange(field, half, step[0], step[1], False)

    one_hot = offset_table(win)
    pos_bias = jnp.einsum(
        "hc,qkc->hqk",
        rel_table.reshape(head_count, span_count * span_count),
        one_hot,
        precision=lax.Precision.HIGHEST,
    )
    pos_bias = jnp.concatenate([pos_bias] * bands, axis=-1)
    labels = jnp.roll(
        mask_ids,
        (
            -(lax.axis_index("row") * tile_rows + step[0]),
            -(lax.axis_index("col") * tile_cols + step[1]),
        ),
        (0, 1),
    )[:tile_rows, :tile_cols]
    labels = labels.reshape(bands, win, tile_cols).transpose(0, 2, 1).reshape(-1)
    band = jnp.arange(tile_rows * tile_cols, dtype=jnp.int32) // (win * tile_cols)
    allowed = (labels[:, None] == labels[None, :]) & (band[:, None] == band[None, :])
    neg = jnp.where(allowed, 0.0, NEG_FILL).astype(jnp.float32)

    heads = 2 if head_count % 2 == 0 else 1
    width = heads * dim
    tokens = tile_rows * tile_cols
    specs = field_specs(tile_cols, tile_rows, half, width)
    smem = pl.BlockSpec(memory_space=pltpu.SMEM)
    out, dgain, dbias = pl.pallas_call(
        functools.partial(attend_kernel, heads=heads, dim=dim, half=half),
        grid=(head_count // heads,),
        in_specs=[smem]
        + specs
        + [
            pl.BlockSpec((2, dim), lambda i: (0, 0)),
            pl.BlockSpec((heads, tokens // bands, tokens), lambda i: (i, 0, 0)),
            pl.BlockSpec((tokens, tokens), lambda i: (0, 0)),
        ],
        out_specs=[
            specs[0],
            pl.BlockSpec((2, dim), lambda i: (0, 0)),
            pl.BlockSpec((heads, tokens // bands, tokens), lambda i: (i, 0, 0)),
        ],
        out_shape=[
            jax.ShapeDtypeStruct(field.shape, jnp.bfloat16),
            jax.ShapeDtypeStruct((2, dim), jnp.float32),
            jax.ShapeDtypeStruct((head_count, tokens // bands, tokens), jnp.float32),
        ],
        name="attend",
    )(step, field, *halos, norm_gains, pos_bias, neg)

    per = tokens // bands
    dbias = sum(dbias[:, :, b * per : (b + 1) * per] for b in range(bands))
    table_local = jnp.einsum("hqk,qkc->hc", dbias, one_hot, precision=lax.Precision.HIGHEST)
    totals = lax.psum((dgain, table_local), AXES)

    back = exchange(out, half, step[0], step[1], True)
    width = 4 * dim if head_count % 4 == 0 else dim
    specs = field_specs(tile_cols, tile_rows, half, width)
    merged = pl.pallas_call(
        functools.partial(merge_kernel, half=half),
        grid=(feature_width // width,),
        in_specs=[smem] + specs,
        out_specs=specs[0],
        out_shape=jax.ShapeDtypeStruct(field.shape, jnp.bfloat16),
        name="merge",
    )(step, out, *back)
    merged = merged.transpose(2, 1, 0, 3)
    return (
        merged[:, :, 0],
        merged[:, :, 1:],
        totals[0],
        totals[1].reshape(head_count, span_count, span_count),
    )


def solution(mesh):
    placed = (P("row", "col", None, None), P("row", "col", None), P(), P(), P(), P())
    return jax.shard_map(
        local,
        mesh=mesh,
        in_specs=placed,
        out_specs=(P("row", "col", None), P("row", "col", None, None), P(), P()),
        check_vma=False,
    )
```

```python
import functools
import math

import jax
import jax.numpy as jnp
from jax import lax
from jax.experimental import pallas as pl
from jax.experimental.pallas import tpu as pltpu
from jax.sharding import PartitionSpec as P

EPSILON = 1e-06
NEG_FILL = -1e30
AXES = ("row", "col")


def offset_table(window_size):
    span_count = 2 * window_size - 1
    places = jnp.arange(window_size * window_size, dtype=jnp.int32)
    row_pos = places % window_size
    col_pos = places // window_size
    code_grid = (row_pos[:, None] - row_pos[None, :] + window_size - 1) * span_count + (
        col_pos[:, None] - col_pos[None, :] + window_size - 1
    )
    codes = jnp.arange(span_count * span_count, dtype=jnp.int32)
    return (code_grid[:, :, None] == codes[None, None, :]).astype(jnp.float32)


def strips_of(field, half, row_dir, col_first, width):
    tile_rows = field.shape[2]
    row_part = slice(0, half) if row_dir > 0 else slice(tile_rows - half, tile_rows)
    col_strip = lax.dynamic_slice_in_dim(field, col_first, width, 1)
    return (col_strip, col_strip[:, :, row_part], field[:, :, row_part])


def send_strips(strips, half, row_step, col_step, col_at):
    rows = lax.axis_size("row")
    cols = lax.axis_size("col")
    col_strip, corner, row_strip = strips
    row_pairs = [(a, (a + row_step) % rows) for a in range(rows)]
    col_pairs = [(a, (a + col_step) % cols) for a in range(cols)]
    both_pairs = [
        (a * cols + b, ((a + row_step) % rows) * cols + (b + col_step) % cols)
        for a in range(rows)
        for b in range(cols)
    ]
    col_strip = lax.ppermute(col_strip, "col", col_pairs)
    row_strip = lax.ppermute(row_strip, "row", row_pairs)
    corner = lax.ppermute(corner, AXES, both_pairs)
    return (row_strip, col_strip, corner)


def total_over(value, axis):
    count = lax.axis_size(axis)
    if count & (count - 1):
        return lax.psum(value, axis)
    reach = 1
    while reach < count:
        value = value + lax.ppermute(value, axis, [(a, a ^ reach) for a in range(count)])
        reach *= 2
    return value


def foreign(position, step, extent):
    return (position < step) | (position >= extent + step)


def merged_column(own, row_halo, col_halo, corner, f, q, lanes, step_row, step_col, half):
    width = col_halo.shape[1]
    tile_cols, tile_rows = own.shape[1], own.shape[2]
    outside = foreign(q, step_col, tile_cols)
    first = jnp.where(step_col > 0, 0, tile_cols - width)
    slot = jnp.clip(q - first, 0, width - 1)
    main = jnp.where(outside, col_halo[f, slot, :, lanes], own[f, q, :, lanes])
    main = main.astype(jnp.float32)
    side = jnp.where(outside, corner[f, slot, :, lanes], row_halo[f, q, :, lanes])
    side = side.astype(jnp.float32)
    side = jnp.concatenate([side] * (tile_rows // half), axis=0)
    row = lax.broadcasted_iota(jnp.int32, main.shape, 0)
    return jnp.where(foreign(row, step_row, tile_rows), side, main)


def attend_kernel(
    steps, own, row_halo, col_halo, corner, gains, bias, neg, out, dgain, dbias, *, heads, dim, half
):
    step_row, step_col = steps[0], steps[1]
    tile_cols, tile_rows = own.shape[1], own.shape[2]
    win = 2 * half
    scale = 1.0 / math.sqrt(dim)

    @pl.when(pl.program_id(0) == 0)
    def _():
        dgain[...] = jnp.zeros_like(dgain)

    where_from = [lax.rem(j + step_col + tile_cols, tile_cols) for j in range(tile_cols)]
    up = lax.rem(tile_rows - step_row, tile_rows)
    down = lax.rem(tile_rows + step_row, tile_rows)
    bands = tile_rows // win
    tokens = tile_rows * tile_cols
    dot = functools.partial(lax.dot_general, preferred_element_type=jnp.float32)
    gain_q, gain_k = gains[0:1, :], gains[1:2, :]

    for h in range(heads):
        lanes = pl.ds(h * dim, dim)
        fields = []
        for f in range(4):
            columns = [
                pltpu.roll(
                    merged_column(
                        own, row_halo, col_halo, corner, f, q, lanes, step_row, step_col, half
                    ),
                    up,
                    0,
                )
                for q in where_from
            ]
            fields.append(
                jnp.concatenate(
                    [c[b * win : (b + 1) * win] for b in range(bands) for c in columns], axis=0
                )
            )

        def normed(x, gain):
            centred = x - jnp.mean(x, axis=-1, keepdims=True)
            variance = jnp.mean(centred * centred, axis=-1, keepdims=True)
            inv = lax.rsqrt(variance + EPSILON)
            hat = centred * inv
            return hat, inv, (hat * gain).astype(jnp.bfloat16)

        q_hat, q_inv, qn = normed(fields[0], gain_q)
        k_hat, k_inv, kn = normed(fields[1], gain_k)
        v = fields[2].astype(jnp.bfloat16)
        cot = fields[3].astype(jnp.bfloat16)
        b = jnp.concatenate([bias[h]] * bands, axis=0)
        s = dot(qn, kn, (((1,), (1,)), ((), ()))) * scale + b + neg[...]
        e = jnp.exp(s - jnp.max(s, axis=-1, keepdims=True))
        p = e / jnp.sum(e, axis=-1, keepdims=True)
        pb = p.astype(jnp.bfloat16)
        att = dot(pb, v, (((1,), (0,)), ((), ())))
        dp = dot(cot, v, (((1,), (1,)), ((), ())))
        ds = p * (dp - jnp.sum(p * dp, axis=-1, keepdims=True))
        dsb = ds.astype(jnp.bfloat16)
        dqn = dot(dsb, kn, (((1,), (0,)), ((), ()))) * scale
        dkn = dot(dsb, qn, (((0,), (0,)), ((), ()))) * scale
        dv = dot(pb, cot, (((0,), (0,)), ((), ())))
        folded = ds[0 : tokens // bands]
        for band in range(1, bands):
            folded = folded + ds[band * (tokens // bands) : (band + 1) * (tokens // bands)]
        dbias[h] = functools.reduce(
            jnp.add,
            [folded[:, w * (tokens // bands) : (w + 1) * (tokens // bands)] for w in range(bands)],
        )

        def norm_back(hat, inv, dn, gain):
            g = dn * gain
            first = jnp.mean(g, axis=-1, keepdims=True)
            second = jnp.mean(g * hat, axis=-1, keepdims=True)
            return inv * (g - first - hat * second), jnp.sum(dn * hat, axis=0, keepdims=True)

        dq, gq = norm_back(q_hat, q_inv, dqn, gain_q)
        dk, gk = norm_back(k_hat, k_inv, dkn, gain_k)
        dgain[...] += jnp.concatenate([gq, gk], axis=0)
        for f, result in enumerate((att, dq, dk, dv)):
            for j, q in enumerate(where_from):
                parts = [
                    result[(bd * tile_cols + j) * win : (bd * tile_cols + j + 1) * win]
                    for bd in range(bands)
                ]
                column = pltpu.roll(jnp.concatenate(parts, axis=0), down, 0)
                out[f, q, :, lanes] = column.astype(jnp.bfloat16)


def merge_kernel(steps, own, row_halo, col_halo, corner, out, *, half):
    lanes = pl.ds(0, own.shape[3])
    for f in range(own.shape[0]):
        for q in range(own.shape[1]):
            out[f, q] = merged_column(
                own, row_halo, col_halo, corner, f, q, lanes, steps[0], steps[1], half
            ).astype(jnp.bfloat16)


def field_specs(tile_cols, tile_rows, half, cols, width):
    shapes = (
        (4, tile_cols, tile_rows, width),
        (4, tile_cols, half, width),
        (4, cols, tile_rows, width),
        (4, cols, half, width),
    )
    return [pl.BlockSpec(shape, lambda i: (0, 0, 0, i)) for shape in shapes]


def attend(step, field, halos, norm_gains, pos_bias, neg, first_head, head_count, dim, half):
    tile_cols, tile_rows, features = field.shape[1:]
    tokens = tile_rows * tile_cols
    per = pos_bias.shape[1]
    heads = 2 if head_count % 2 == 0 else 1
    specs = field_specs(tile_cols, tile_rows, half, halos[1].shape[1], heads * dim)
    start = first_head // heads
    return pl.pallas_call(
        functools.partial(attend_kernel, heads=heads, dim=dim, half=half),
        grid=(head_count // heads,),
        in_specs=[pl.BlockSpec(memory_space=pltpu.SMEM)]
        + specs
        + [
            pl.BlockSpec((2, dim), lambda i: (0, 0)),
            pl.BlockSpec((heads, per, tokens), lambda i: (i + start, 0, 0)),
            pl.BlockSpec((tokens, tokens), lambda i: (0, 0)),
        ],
        out_specs=[
            specs[0],
            pl.BlockSpec((2, dim), lambda i: (0, 0)),
            pl.BlockSpec((heads, per, per), lambda i: (i, 0, 0)),
        ],
        out_shape=[
            jax.ShapeDtypeStruct(field.shape, jnp.bfloat16),
            jax.ShapeDtypeStruct((2, dim), jnp.float32),
            jax.ShapeDtypeStruct((head_count, per, per), jnp.float32),
        ],
        cost_estimate=pl.CostEstimate(
            flops=14 * head_count * tokens * tokens * dim * 12,
            bytes_accessed=16 * field.size,
            transcendentals=head_count * tokens * tokens,
        ),
        name="attend",
    )(step, field, *halos, norm_gains, pos_bias, neg)


def merge(step, fields, halos, half):
    _, tile_cols, tile_rows, features = fields.shape
    width = features // 3 if features % 384 == 0 else features
    specs = field_specs(tile_cols, tile_rows, half, halos[1].shape[1], width)
    return pl.pallas_call(
        functools.partial(merge_kernel, half=half),
        grid=(features // width,),
        in_specs=[pl.BlockSpec(memory_space=pltpu.SMEM)] + specs,
        out_specs=specs[0],
        out_shape=jax.ShapeDtypeStruct(fields.shape, jnp.bfloat16),
        cost_estimate=pl.CostEstimate(
            flops=4 * fields.size, bytes_accessed=8 * fields.size, transcendentals=0
        ),
        name="merge",
    )(step, fields, *halos)


def whole_pass(
    groups, norm_gains, rel_table, mask_ids, step, *, row_dir, col_dir, width, half, head_count, dim
):
    tile_cols, tile_rows = groups[0].shape[1:3]
    span_count = rel_table.shape[1]
    win = 2 * half
    bands = tile_rows // win
    tokens = tile_rows * tile_cols
    first_col = jnp.where(step[1] > 0, 0, tile_cols - width)
    strips = [strips_of(g, half, row_dir, first_col, width) for g in groups]

    halos = []
    for g in range(len(groups)):
        if halos:
            strips[g], halos[-1] = lax.optimization_barrier((strips[g], halos[-1]))
        halos.append(send_strips(strips[g], half, -row_dir, -col_dir, first_col))

    one_hot = offset_table(win)
    pos_bias = jnp.einsum(
        "hc,qkc->hqk",
        rel_table.reshape(head_count, span_count * span_count),
        one_hot,
        precision=lax.Precision.HIGHEST,
    )
    pos_bias = jnp.concatenate([pos_bias] * bands, axis=-1)
    labels = jnp.roll(
        mask_ids,
        (
            -(lax.axis_index("row") * tile_rows + step[0]),
            -(lax.axis_index("col") * tile_cols + step[1]),
        ),
        (0, 1),
    )[:tile_rows, :tile_cols]
    labels = labels.reshape(bands, win, tile_cols).transpose(0, 2, 1).reshape(-1)
    band = jnp.arange(tokens, dtype=jnp.int32) // (win * tile_cols)
    allowed = (labels[:, None] == labels[None, :]) & (band[:, None] == band[None, :])
    neg = jnp.where(allowed, 0.0, NEG_FILL).astype(jnp.float32)

    per_group = head_count // len(groups)
    outs, gains, biases, backs = [], [], [], []
    for g, group in enumerate(groups):
        out, gain, bias = attend(
            step, group, halos[g], norm_gains, pos_bias, neg, g * per_group, per_group, dim, half
        )
        outs.append(out)
        gains.append(gain)
        biases.append(bias)
        backs.append(
            send_strips(
                strips_of(out, half, row_dir, first_col, width), half, row_dir, col_dir, first_col
            )
        )
    table = jnp.einsum(
        "hqk,qkc->hc", jnp.concatenate(biases, axis=0), one_hot, precision=lax.Precision.HIGHEST
    )
    sums = jnp.concatenate([sum(gains).reshape(-1), table.reshape(-1)])
    count = sums.shape[0]
    sums = jnp.pad(sums, (0, -count % 1024)).reshape(-1, 128)
    sums = total_over(total_over(sums, "col"), "row").reshape(-1)[:count]
    d_gains = sums[: 2 * dim].reshape(2, dim)
    d_table = sums[2 * dim :].reshape(head_count, span_count, span_count)
    merged = [merge(step, outs[g], backs[g], half) for g in range(len(groups))]
    return (merged, d_gains, d_table)


def local(qkv, cotangent, norm_gains, rel_table, shifts, mask_ids):
    feature_width = qkv.shape[3]
    head_count = rel_table.shape[0]
    dim = feature_width // head_count
    win = (rel_table.shape[1] + 1) // 2
    half = win // 2
    step = jnp.where(shifts <= half, shifts, shifts - win).astype(jnp.int32)
    parts = 2 if head_count % 4 == 0 else 1
    cut = feature_width // parts
    groups = [
        jnp.concatenate([qkv, cotangent[:, :, None]], axis=2)[..., g * cut : (g + 1) * cut].transpose(
            2, 1, 0, 3
        )
        for g in range(parts)
    ]
    col_dirs = (1,) if lax.axis_size("col") <= 2 else (1, -1)
    branches = [
        functools.partial(
            whole_pass,
            row_dir=row_dir,
            col_dir=col_dir,
            width=width,
            half=half,
            head_count=head_count,
            dim=dim,
        )
        for row_dir in (1, -1)
        for col_dir in col_dirs
        for width in range(1, half + 1)
    ]
    index = (
        jnp.where(step[0] > 0, 0, len(col_dirs) * half)
        + jnp.where(step[1] > 0, 0, (len(col_dirs) - 1) * half)
        + jnp.maximum(jnp.abs(step[1]), 1)
        - 1
    )
    merged, d_gains, d_table = lax.switch(
        index, branches, groups, norm_gains, rel_table, mask_ids, step
    )
    merged = jnp.concatenate(merged, axis=-1).transpose(2, 1, 0, 3)
    return (merged[:, :, 0], merged[:, :, 1:], d_gains, d_table)


def solution(mesh):
    placed = (P("row", "col", None, None), P("row", "col", None), P(), P(), P(), P())
    return jax.shard_map(
        local,
        mesh=mesh,
        in_specs=placed,
        out_specs=(P("row", "col", None), P("row", "col", None, None), P(), P()),
        check_vma=False,
    )
```
